32 devices in a mesh: grp: 2 (over y), src: 4 (over z), chan: 2 (over x), row: 2 (over core).
Axes of the slice: x: 2, y: 2, z: 4, core: 2. Of those that a mesh axis runs over, the one named last changes fastest.
Arguments:
- features: bfloat16 [64, 128, 512], P('chan', ('grp', 'row'), 'src'), parts along dimension 1, may hold values from -6 to 6
- layout: int32 [128, 512], P(('grp', 'row'), 'chan'), parts along dimension 0, may hold values 0 or 1
- conv_weight: bfloat16 [4, 4, 9, 64, 64], P('src'), may hold values from -0.25 to 0.25
- conv_bias: float32 [4, 4, 64], P('src'), may hold values from -2 to 2
- head_weight: bfloat16 [4, 64, 16], P('src'), may hold values from -0.75 to 0.75
- transmission: float32 [4, 16], P('src'), may hold values from -3 to 3
- point_weight: float32 [128], replicated, may hold values from 0.1 to 1
- assignment: int32 [128, 1], replicated, may hold values from 0 to 3
Outputs:
- intensity: float32 [8, 4, 32, 512], P(None, ('grp', 'row'), 'src', 'chan'), parts along dimension 1
The draws below stay inside these ranges and needn't reach their ends.
There are 2 independent parts, one for each index of `grp`. The reference program is written for one: setup_inputs(seed, part) draws one part's arguments, and reference() takes and returns one part's arrays. A program takes and returns all parts, laid end to end along the dimension named above; an argument that names none is the same for every part. Nothing has to cross between parts.
Inputs may be any that keep to these rules, and one draw needn't show every extreme that they name: `assignment`: every cluster is named by at least one point.
All inputs are finite; a program needn't handle non-finite values. No bound on the sum of `layout` on one device may be relied on, other than what follows from the above.
Results may differ from the reference program's by a relative error of at most 0.009.
Values may be sent and summed in bfloat16 or wider, within the bound.
A program may use at most 64 MiB of HBM per device.

```python
import math
import jax
import jax.numpy as jnp
from jax import lax

C = 64
W = 512
STRIP = 32
LAYERS = 4
K = 8
S = 4
POINTS = 128
H = 64
N_ROW = 2


def with_ends(values, key, smallest, high):
    extent = values.shape
    index_at = [jax.random.randint(jax.random.fold_in(key, axis), (), 0, extent[axis]) for axis in range(len(extent))]
    values = values.at[tuple(index_at)].set(smallest)
    longest = extent.index(max(extent))
    index_at[longest] = (index_at[longest] + 1) % extent[longest]
    return values.at[tuple(index_at)].set(high)


def levels(key, dims, shards, low, high):
    loudness = 1.0
    for position, blocks in shards:
        heights = jax.random.uniform(jax.random.fold_in(jax.random.fold_in(key, 6), position), (blocks,), jnp.float32, low / len(shards), high / len(shards))
        loudness = loudness * jnp.repeat(jnp.exp(heights), dims[position] // blocks).reshape((-1,) + (1,) * (len(dims) - 1 - position))
    return loudness


def distinct(own_key, rows, amount, top, lift):
    ranking = jax.random.permutation(jax.random.fold_in(own_key, 1), amount)
    boost = ranking
    for power in range(3):
        boost = boost * boost // amount
    boost = boost * lift // amount
    lots = jax.random.randint(jax.random.fold_in(own_key, 2), (rows, amount), 0, 4096) + boost
    fixed_rows = jax.random.permutation(jax.random.fold_in(own_key, 3), rows)[jnp.arange(amount) % rows]
    lots = jnp.where(jnp.arange(rows)[:, None] == fixed_rows[None, :], 1 << 14, lots)
    priority = lots * amount + jnp.arange(amount)
    return lax.top_k(priority.astype(jnp.int32), top)[1].astype(jnp.int32)


def noise(key, shape, scale, most, pieces=(), kind=jnp.bfloat16):
    gain = levels(key, shape, pieces, -0.22, 0.18) if pieces else 1.0
    array = jax.random.normal(key, shape, jnp.float32) * scale * gain
    return jnp.minimum(jnp.maximum(array, -most), most).astype(kind)


def setup_inputs(seed: int = 0, part: int = 0) -> dict:
    seeds = jax.random.split(jax.random.key(seed), 9)
    part_keys = jax.random.split(jax.random.fold_in(seeds[8], part), 9)
    features = noise(part_keys[0], (C, H, W), 1.0, 6.0, ((0, 2), (1, 2), (2, 4)))
    layout = with_ends((jax.random.randint(part_keys[1], (H, W), 0, 2) < 1).astype(jnp.int32), jax.random.fold_in(part_keys[1], 1), 0, 1)
    conv_weight = noise(seeds[2], (S, LAYERS, 9, C, C), (9 * C) ** -0.5, 0.25, ((0, 4),))
    conv_bias = noise(seeds[3], (S, LAYERS, C), 0.3, 2.0, ((0, 4),), jnp.float32)
    head_weight = noise(seeds[4], (S, C, 2 * K), C ** -0.5, 0.75, ((0, 4),))
    transmission = noise(seeds[5], (S, 2 * K), 0.5, 3.0, ((0, 4),), jnp.float32)
    point_weight = jnp.clip(jnp.exp(jax.random.uniform(seeds[6], (POINTS,), jnp.float32, math.log(0.1), math.log(1.0))), 0.1, 1.0)
    assignment = distinct(seeds[7], POINTS, S, 1, 2048)
    return {"features": features, "layout": layout, "conv_weight": conv_weight, "conv_bias": conv_bias, "head_weight": head_weight, "transmission": transmission, "point_weight": point_weight, "assignment": assignment}


def advance(hidden, padded, weights, biases, dilation):
    tile_rows, tile_cols = hidden.shape[1], hidden.shape[2]
    summed = jnp.zeros(hidden.shape, jnp.float32) + biases.astype(jnp.float32)[:, None, None]
    for tap_index in range(9):
        row_off = (tap_index // 3) * dilation
        col_off = (tap_index % 3) * dilation
        window = padded[:, row_off:row_off + tile_rows, col_off:col_off + tile_cols].astype(jnp.float32)
        summed = summed + jnp.einsum("io,ihw->ohw", weights[tap_index].astype(jnp.float32), window)
    return (hidden.astype(jnp.float32) + jax.nn.gelu(summed, approximate=True)).astype(jnp.bfloat16)


def reference(features, layout, conv_weight, conv_bias, head_weight, transmission, point_weight, assignment):
    chosen = (assignment[:, 0][None, :] == jnp.arange(S, dtype=jnp.int32)[:, None]).astype(jnp.float32)
    cluster_weight = jnp.sum(chosen * point_weight[None, :], axis=1) / jnp.sum(point_weight)
    mask_map = layout.astype(jnp.float32)

    def one_cluster(running, inputs):
        weights, biases, head_map, shift_term, cluster_share = inputs
        hidden = features
        for layer_index in range(LAYERS):
            dilation = 2 ** layer_index
            padded = jnp.pad(hidden, ((0, 0), (dilation, dilation), (dilation, dilation)))
            hidden = advance(hidden, padded, weights[layer_index], biases[layer_index], dilation)
        field_map = jnp.einsum("ihw,ik->khw", hidden.astype(jnp.float32), head_map.astype(jnp.float32))
        field_map = field_map + mask_map[None] * shift_term[:, None, None]
        power_map = field_map[:K] ** 2 + field_map[K:] ** 2
        return running + cluster_share * power_map, None

    summed, leftover = lax.scan(one_cluster, jnp.zeros((K, H, W), jnp.float32), (conv_weight, conv_bias, head_weight, transmission, cluster_weight))
    return summed.reshape(K, N_ROW, STRIP, W)
```

```python
import functools
import math

import jax
import jax.numpy as jnp
from jax import lax
from jax.experimental import pallas as pl
from jax.experimental.pallas import tpu as pltpu
from jax.sharding import PartitionSpec as P


def with_halo(block, sides, width):
    for axis, dim in sides:
        count = lax.axis_size(axis)
        forward = [(i, i + 1) for i in range(count - 1)]
        backward = [(target, source) for source, target in forward]
        low = lax.ppermute(
            lax.slice_in_dim(block, block.shape[dim] - width, None, axis=dim), axis, forward
        )
        high = lax.ppermute(lax.slice_in_dim(block, 0, width, axis=dim), axis, backward)
        block = jnp.concatenate([low, block, high], axis=dim)
    return block


def advance(core_cells, padded, weights, biases, dilation):
    tile_rows, tile_cols = (core_cells.shape[1], core_cells.shape[2])
    kernel = weights.reshape(3, 3, weights.shape[1], weights.shape[2])
    window = padded[:, : tile_rows + 2 * dilation, : tile_cols + 2 * dilation]
    summed = lax.conv_general_dilated(
        window[None],
        kernel,
        (1, 1),
        "VALID",
        rhs_dilation=(dilation, dilation),
        dimension_numbers=("NCHW", "HWIO", "NCHW"),
        preferred_element_type=jnp.float32,
    )[0]
    summed = summed + biases[:, None, None]
    return (core_cells.astype(jnp.float32) + jax.nn.gelu(summed, approximate=True)).astype(
        jnp.bfloat16
    )


def by_cluster(
    features, layout, conv_weight, conv_bias, head_weight, transmission, point_weight, assignment
):
    channels = lax.all_gather(features, "chan", axis=0, tiled=True)
    full_cache = lax.all_gather(channels, "src", axis=2, tiled=True)
    column_width = full_cache.shape[2] // lax.axis_size("chan")
    tile_cache = lax.dynamic_slice_in_dim(
        full_cache, lax.axis_index("chan") * column_width, column_width, 2
    )
    weights = conv_weight[0]
    biases = conv_bias[0]
    hidden = tile_cache
    for layer_index in range(weights.shape[0]):
        dilation = 2**layer_index
        padded = with_halo(hidden, (("chan", 2), ("row", 1)), dilation)
        hidden = advance(hidden, padded, weights[layer_index], biases[layer_index], dilation)
    field_map = jnp.einsum(
        "ihw,ik->khw", hidden, head_weight[0], preferred_element_type=jnp.float32
    )
    field_map = field_map + layout.astype(jnp.float32)[None] * transmission[0][:, None, None]
    planes = field_map.shape[0] // 2
    power_map = field_map[:planes] ** 2 + field_map[planes:] ** 2
    chosen = assignment[:, 0] == lax.axis_index("src")
    cluster_share = jnp.sum(jnp.where(chosen, point_weight, jnp.zeros((), jnp.float32))) / jnp.sum(
        point_weight
    )
    summed = lax.psum_scatter(
        (power_map * cluster_share).astype(jnp.bfloat16), "src", scatter_dimension=1, tiled=True
    ).astype(jnp.float32)
    return summed[:, None]


def gelu_of_half(v):
    c = 2.0 * math.sqrt(2.0 / math.pi)
    return v + v * jnp.tanh(v * (c + (c * 4.0 * 0.044715) * (v * v)))


def half_lanes(shape):
    return lax.broadcasted_iota(jnp.int32, shape, len(shape) - 1) < shape[-1] // 2


def pair_up(h, d, segs):
    n, sub, lanes = h.shape
    low = half_lanes((1, sub, lanes))
    if d * segs < sub:
        first = lax.broadcasted_iota(jnp.int32, (1, sub, lanes), 1) < sub // 2
        other = pltpu.roll(pltpu.roll(h, sub // 2, 1), lanes // 2, 2)
        return jnp.where(first == low, h, other)
    g = d * segs // sub
    turned = pltpu.roll(h, lanes // 2, 2)
    groups = n // g
    at = lambda x, m: x[m * g : (m + 1) * g]
    out = []
    for i in range((groups + 2) // 2):
        u, v = 2 * i - 1, 2 * i
        if i == 0:
            out += [at(turned, v), at(h, v)]
        elif v == groups:
            out += [at(h, u), at(turned, u)]
        else:
            out += [jnp.where(low, at(h, u), at(turned, v)), jnp.where(low, at(turned, u), at(h, v))]
    return jnp.concatenate(out, axis=0)


def shift_segment(h, segs, down):
    sub = lax.broadcasted_iota(jnp.int32, (1,) + h.shape[1:], 1) % segs
    if down:
        return jnp.where(sub == 0, 0.0, pltpu.roll(h, 1, 1))
    return jnp.where(sub == segs - 1, 0.0, pltpu.roll(h, h.shape[1] - 1, 1))


MESH = pl.DeviceIdType.MESH
CHUNKS = 2


def xor(s, k):
    total = s
    bit = 1
    while bit <= k:
        if k & bit:
            total = total + bit - 2 * bit * ((s // bit) % 2)
        bit *= 2
    return total


def pixel_kernel(
    layers, n_src, t_ref, w_ref, h_ref, tr_ref, b_ref, m_ref, pw_ref, as_ref, o_ref, *scratch
):
    first, bufs = scratch[0], (scratch[1 : layers + 1], scratch[layers + 1 : 2 * layers + 1])
    got, wraw, pbuf, mbuf, wide, acc, sbuf, obuf, stage, rowbuf = scratch[2 * layers + 1 : 2 * layers + 11]
    fs, fr, es, er, ws, wr, vs, vr, ps, pr, ms, mr, os, orr, lw = scratch[2 * layers + 11 :]
    s, c, r = (lax.axis_index(a) for a in ("src", "chan", "row"))
    lanes = t_ref.shape[2]
    half_rows = t_ref.shape[1]
    rows = 4 * half_rows
    piece = t_ref.shape[0] // 8
    here = 2 * c + r
    side = c

    ch = lanes // 2
    planes2 = h_ref.shape[0]
    ia = lax.broadcasted_iota(jnp.int32, (planes2, planes2), 0)
    ib = lax.broadcasted_iota(jnp.int32, (planes2, planes2), 1)
    column = jnp.sum(jnp.where(ia == ib, tr_ref[...], 0.0), axis=1, keepdims=True)
    pbuf[0, :planes2, :] = jnp.concatenate(
        [h_ref[...].astype(jnp.float32), jnp.broadcast_to(column, (planes2, ch))], axis=1)
    bias_half = 0.5 * b_ref[...]
    pbuf[0, planes2 : planes2 + layers, :] = jnp.concatenate([bias_half, bias_half], axis=1)

    barrier = pltpu.get_barrier_semaphore()
    for s1 in range(n_src):
        for c1 in range(2):
            for r1 in range(2):
                @pl.when(jnp.logical_not((s == s1) & (c == c1) & (r == r1)))
                def _():
                    pl.semaphore_signal(
                        barrier, inc=1, device_id={"src": s1, "chan": c1, "row": r1},
                        device_id_type=MESH,
                    )
    pl.semaphore_wait(barrier, 4 * n_src - 1)

    def remote(src, dst, a, b, s1, c1, r1):
        return pltpu.make_async_remote_copy(
            src_ref=src, dst_ref=dst, send_sem=a, recv_sem=b,
            device_id={"src": s1, "chan": c1, "row": r1}, device_id_type=MESH,
        )

    def main_copy(c1, r1):
        return (
            t_ref.at[pl.ds(piece * (3 * c1 + 2 * r1), 3 * piece)],
            got.at[here, pl.ds(piece * (1 - c1), 3 * piece)],
        )

    def edge_copy(c1, r1):
        at = 7 * (1 - c1) if c1 == r1 else 1 + 5 * c1
        return t_ref.at[pl.ds(piece * at, piece)], got.at[here, pl.ds(piece * 3 * c1, piece)]

    def each(act):
        for c1 in (0, 1):
            for r1 in (0, 1):
                k = 2 * c1 + r1
                me = (c == c1) & (r == r1)
                act(c1, r1, k, me)

    def send_main(c1, r1, k, me):
        src, dst = main_copy(c1, r1)
        pl.when(jnp.logical_not(me))(
            lambda: remote(src, dst, fs.at[k], fr.at[here], s, c1, r1).start())
        pl.when(me)(lambda: pltpu.make_async_copy(src, dst, fr.at[here]).start())

    def edge_step(c1):
        return 1 - 2 * c1

    def send_edge(c1, r1, k, me):
        src, dst = edge_copy(c1, r1)
        if c1 == r1:
            s1 = s + edge_step(c1)
            pl.when((s1 >= 0) & (s1 < n_src))(
                lambda: remote(src, dst, es.at[k], er.at[here], s1, c1, r1).start())
        else:
            pl.when(jnp.logical_not(me))(
                lambda: remote(src, dst, es.at[k], er.at[here], s, c1, r1).start())
            pl.when(me)(lambda: pltpu.make_async_copy(src, dst, er.at[here]).start())

    def send_mask(c1, r1, k, me):
        src, dst = m_ref.at[k], mbuf.at[r]
        owner = c == (2 * s) // n_src
        pl.when(owner & jnp.logical_not(me))(
            lambda: remote(src, dst, ms.at[k], mr.at[r], s, c1, r1).start())
        pl.when(owner & me)(lambda: pltpu.make_async_copy(src, dst, mr.at[r]).start())

    each(send_main)
    each(send_edge)

    def wz(k):
        return remote(w_ref.at[r], wraw.at[k, r], ws.at[k], wr.at[k], xor(s, k), c, r)

    def pz(k):
        return remote(pbuf.at[0], pbuf.at[k], ps.at[k], pr.at[k], xor(s, k), c, r)

    for k in range(1, n_src):
        pz(k).start()
        wz(k).start()
    each(send_mask)
    own_w = pltpu.make_async_copy(w_ref, wraw.at[0], lw)
    own_w.start()

    for k in range(n_src):
        for l in range(layers):
            for at, cut in ((0, lanes), (12 * ch, 0)):
                wide[k, l, at : at + 4 * ch, cut : cut + lanes] = jnp.zeros((4 * ch, lanes), wide.dtype)
    outside = ((here == 0) & (s == 0)) | ((here == 3) & (s == n_src - 1))

    @pl.when(outside)
    def _():
        for k in range(4):
            got[k, pl.ds(piece * 3 * side, piece)] = jnp.zeros((piece,) + got.shape[2:], got.dtype)

    def build(k):
        low = lax.broadcasted_iota(jnp.int32, (ch, lanes), 1) < ch
        per = layers // 2
        for l in range(layers):
            raw = lambda i: wraw[k, l // per, (l % per) * 5 + i].astype(jnp.float32) * 0.5
            firsts = [raw(b) for b in range(3)]
            q0, q1 = raw(3), raw(4)
            seconds = [q0, pltpu.roll(q0, ch, 1), q1]
            for b in range(3):
                w10, w2 = firsts[b], seconds[b]
                swap = pltpu.roll(w10, ch, 1)
                blocks = [
                    w10,
                    jnp.where(low, w2, swap),
                    jnp.where(low, 0.0, pltpu.roll(w2, ch, 1)),
                    jnp.where(low, swap, 0.0),
                ]
                for j in range(4):
                    v = blocks[j].astype(wide.dtype)
                    for ic in range(2):
                        at = (b + ic) * 4 * ch + j * ch
                        wide[k, l, at : at + ch, ic * lanes : (ic + 1) * lanes] = v

    own_w.wait()
    build(0)

    def wait_main(c1, r1, k, me):
        src, _ = main_copy(0, 0)
        dst = got.at[k, pl.ds(piece * (1 - side), 3 * piece)]
        pl.when(jnp.logical_not(me))(
            lambda: remote(src, dst, fs.at[k], fr.at[k], s, c1, r1).wait_recv())
        pl.when(me)(lambda: pltpu.make_async_copy(src, dst, fr.at[k]).wait())

    def wait_edge(c1, r1, k, me):
        src, _ = edge_copy(0, 0)
        dst = got.at[k, pl.ds(piece * 3 * side, piece)]
        far = c == r
        inside = jnp.logical_not(outside)
        pl.when(jnp.where(far, inside, jnp.logical_not(me)))(
            lambda: remote(src, dst, es.at[k], er.at[k], s, c1, r1).wait_recv())
        pl.when(jnp.logical_not(far) & me)(
            lambda: pltpu.make_async_copy(src, dst, er.at[k]).wait())

    each(wait_main)
    each(wait_edge)
    q = ch // 2
    span = 2**layers
    segs = rows // span
    slots = got.shape[1]
    own_cols = 2 * slots - 2 * span
    rin = lax.broadcasted_iota(jnp.int32, (2 * lanes, 2 * lanes), 0)
    rout = lax.broadcasted_iota(jnp.int32, (2 * lanes, 2 * lanes), 1)
    want = (rout // q % 2) * lanes + (rout // ch % 2) * ch + (rout // lanes) * q + rout % q
    place = jnp.where(rin == want, 1.0, 0.0).astype(t_ref.dtype)
    for r1 in range(2):
        lhs = jnp.concatenate(
            [got[2 * c1 + r1].reshape(slots * half_rows, lanes) for c1 in range(2)], axis=1)
        v = jnp.dot(lhs, place, preferred_element_type=jnp.float32)
        for yp in range(2):
            stage[2 * r1 + yp] = v[:, yp * lanes : (yp + 1) * lanes]
    mrows = slots * segs
    rowbuf[0:8, :] = jnp.zeros((8, lanes), jnp.float32)
    rowbuf[8 + span * mrows : 16 + span * mrows, :] = jnp.zeros((8, lanes), jnp.float32)
    for r1 in range(2):
        for y2 in range(half_rows):
            for yp in range(2):
                y = 2 * y2 + yp
                at = 8 + (y % span) * mrows + r1 * (segs // 2) + y // span
                rowbuf[pl.ds(at, slots, stride=segs), :] = stage[
                    2 * r1 + yp, pl.ds(y2, slots, stride=half_rows), :]
    low_lanes = half_lanes((1, 8, lanes))
    as_tiles = lambda v: v.reshape(-1, 8, lanes)
    for y in range(span):
        at = 8 + y * mrows
        own = as_tiles(rowbuf[at : at + mrows, :])
        near = jnp.where(
            low_lanes, as_tiles(rowbuf[at + segs : at + segs + mrows, :]),
            as_tiles(rowbuf[at - segs : at - segs + mrows, :]))
        places = [(y, own, near)]
        if y == span - 1:
            places.append((-1, shift_segment(own, segs, True), shift_segment(near, segs, True)))
        if y == 0:
            places.append((span, shift_segment(own, segs, False), shift_segment(near, segs, False)))
        for yy, a, b in places:
            first[yy + 1, :, :lanes] = a.reshape(mrows, lanes).astype(first.dtype)
            first[yy + 1, :, lanes:] = b.reshape(mrows, lanes).astype(first.dtype)

    at_left = (here == 0) & (s == 0)
    at_right = (here == 3) & (s == n_src - 1)
    for r1 in range(2):
        for_self = (c == (2 * s) // n_src) & (r == r1)
        pl.when(jnp.logical_not(for_self))(
            lambda: remote(m_ref.at[0], mbuf.at[r1], ms.at[0], mr.at[r1], s, c, r).wait_recv())
        pl.when(for_self)(
            lambda: pltpu.make_async_copy(m_ref.at[0], mbuf.at[r1], mr.at[r1]).wait())

    def share_copy(k):
        return remote(wraw.at[k, r], wraw.at[k, r], vs.at[k], vr.at[k], s, c, 1 - r)

    total = jnp.sum(pw_ref[...], axis=1, keepdims=True)

    def store_next(dst, h, y, d):
        wider = 2 * d
        places = [(y, h)]
        if y >= span - wider:
            places.append((y - span, shift_segment(h, segs, True)))
        if y < wider:
            places.append((y + span, shift_segment(h, segs, False)))
        for yy, v in places:
            v = pair_up(v, d, segs)
            n = v.shape[0]
            out = (slots // 2 - own_cols // 4) * segs // 8
            v = jnp.concatenate(
                [jnp.where(at_left, 0.0, v[:out]), v[out : n - out], jnp.where(at_right, 0.0, v[n - out :])],
                axis=0)
            g = wider * segs // 8
            near = jnp.where(low_lanes, v[2 * g :], v[: n - 2 * g])
            own = v[g : n - g]
            dst[yy + wider, :, :lanes] = own.reshape(-1, lanes).astype(dst.dtype)
            dst[yy + wider, :, lanes:] = near.reshape(-1, lanes).astype(dst.dtype)

    def multiply(k, l, ys):
        d = 2**l
        src = first if l == 0 else bufs[k % 2][l - 1]
        lhs = jnp.concatenate(
            [jnp.concatenate([src[y + j * d] for y in ys], axis=0) for j in range(4)], axis=1)
        return jnp.dot(lhs, wide[k, l], preferred_element_type=jnp.float32)

    def activate(k, l, ys, out):
        d = 2**l
        src = first if l == 0 else bufs[k % 2][l - 1]
        dst = bufs[k % 2][l]
        n = src.shape[1]
        bias = pbuf[k, 2 * q2 + l : 2 * q2 + l + 1, :]
        for i, y in enumerate(ys):
            for e in range(2):
                z = out[i * n : (i + 1) * n, e * lanes : (e + 1) * lanes] + bias
                yy = y + e * d
                h = src[yy + d, :, :lanes].astype(jnp.float32) + gelu_of_half(z)
                if l + 1 < layers:
                    store_next(dst, h.reshape(-1, 8, lanes), yy, d)
                else:
                    dst[yy * n : (yy + 1) * n, :] = h

    def finish(k, cid):
        share = jnp.sum(jnp.where(as_ref[...] == cid, pw_ref[...], 0.0), axis=1, keepdims=True) / total
        final = bufs[k % 2][layers - 1]
        n = final.shape[0] // span
        head = pbuf[k, : 2 * q2, :]
        low = lax.broadcasted_iota(jnp.int32, head.shape, 1) < ch
        h_lo = jnp.where(low, head, 0.0)
        h_hi = jnp.where(low, 0.0, pltpu.roll(head, ch, 1))
        tcol = head[:, ch : ch + 1]
        hw = jnp.concatenate([h_lo[:q2], h_hi[:q2], h_lo[q2:], h_hi[q2:]], axis=0).astype(jnp.bfloat16)
        tr = jnp.concatenate([tcol[:q2], tcol[:q2], tcol[q2:], tcol[q2:]], axis=0)
        per = rows // 16
        for g in range(rows // 8):
            at = 8 * (g % 2) * n + g // 2
            block = jnp.concatenate(
                [final[pl.ds(at + b * n, n // segs, stride=segs), :] for b in range(8)], axis=0
            ).astype(jnp.bfloat16)
            field = lax.dot_general(
                hw, block, (((1,), (1,)), ((), ())), preferred_element_type=jnp.float32)
            m = mbuf[g // per, 2 * (g % per) : 2 * (g % per) + 2]
            mm = jnp.concatenate(
                [jnp.broadcast_to(m[i : i + 1], (q2, m.shape[1])) for i in (0, 1, 0, 1)], axis=0)
            field = field + mm * tr
            power = (field[: 2 * q2] ** 2 + field[2 * q2 :] ** 2) * share
            if k == 0:
                acc[g] = power
            else:
                acc[g] = acc[g] + power

    q2 = h_ref.shape[0] // 2

    def take(k):
        wz(k).wait_recv()
        share_copy(k).start()

    def receive(k):
        remote(
            wraw.at[k, 1 - r], wraw.at[k, 1 - r], vs.at[k], vr.at[k], s, c, 1 - r
        ).wait_recv()
        pz(k).wait_recv()
        build(k)

    take(1)
    receive(1)
    for k0 in range(0, n_src, 2):
        pending = None
        for l in range(layers):
            d = 2**l
            tops = [y for y in range(span) if y % (2 * d) < d]
            step = len(tops) // CHUNKS
            for k in (k0, k0 + 1):
                for i in range(CHUNKS):
                    ys = tops[i * step : (i + 1) * step]
                    out = multiply(k, l, ys)
                    if pending:
                        activate(*pending)
                    pending = (k, l, ys, out)
            if k0 + 2 < n_src and l == layers - 2:
                for k in (k0 + 2, k0 + 3):
                    take(k)
        activate(*pending)
        for k in (k0, k0 + 1):
            finish(k, xor(s, k))
        if k0 + 2 < n_src:
            for k in (k0 + 2, k0 + 3):
                receive(k)

    pin = lax.broadcasted_iota(jnp.int32, (2 * lanes, 2 * lanes), 0)
    pout = lax.broadcasted_iota(jnp.int32, (2 * lanes, 2 * lanes), 1)
    column = pout % own_cols
    half = span // 2
    source = (
        (column // half % 2) * lanes + pout // own_cols * (own_cols // 2)
        + column // span * half + column % half)
    order = jnp.where(pin == source, 1.0, 0.0).astype(jnp.bfloat16)
    both = jnp.concatenate(
        [jnp.concatenate([acc[g, :q2], acc[g, q2:]], axis=1) for g in range(rows // 8)], axis=0)
    sbuf[...] = jnp.dot(
        both.astype(jnp.bfloat16), order, preferred_element_type=jnp.float32
    ).reshape(sbuf.shape)

    c2 = (2 * s) // n_src
    slot = 4 * (s % 2) + here

    def outgoing(act):
        for s1 in range(n_src):
            for r1 in range(2):
                k = 2 * s1 + r1
                src = sbuf.at[n_src * r1 + s1]
                me = (s == s1) & (c == c2) & (r == r1)
                act(s1, r1, k, src, me)

    def send_out(s1, r1, k, src, me):
        dst = obuf.at[slot]
        pl.when(jnp.logical_not(me))(
            lambda: remote(src, dst, os.at[k], orr.at[slot], s1, c2, r1).start())
        pl.when(me)(lambda: pltpu.make_async_copy(src, dst, orr.at[slot]).start())

    outgoing(send_out)
    mine = c == c2
    for k in range(2 * n_src):
        me = mine & (slot == k)
        src = sbuf.at[0]
        pl.when(jnp.logical_not(me))(
            lambda: remote(src, obuf.at[k], os.at[k], orr.at[k], s, c, r).wait_recv())
        pl.when(me)(lambda: pltpu.make_async_copy(src, obuf.at[k], orr.at[k]).wait())
    for b in range(8):
        o_ref[:, b, :] = jnp.concatenate(
            [obuf[k, :, b * own_cols : (b + 1) * own_cols] for k in range(2 * n_src)], axis=1)

    def sent_main(c1, r1, k, me):
        src, dst = main_copy(c1, r1)
        pl.when(jnp.logical_not(me))(
            lambda: remote(src, dst, fs.at[k], fr.at[here], s, c1, r1).wait_send())

    def sent_edge(c1, r1, k, me):
        src, dst = edge_copy(c1, r1)
        s1 = s + edge_step(c1)
        gone = (s1 >= 0) & (s1 < n_src) if c1 == r1 else jnp.logical_not(me)
        pl.when(gone)(lambda: remote(src, dst, es.at[k], er.at[here], s, c1, r1).wait_send())

    def sent_mask(c1, r1, k, me):
        owner = c == (2 * s) // n_src
        pl.when(owner & jnp.logical_not(me))(
            lambda: remote(m_ref.at[k], mbuf.at[r], ms.at[k], mr.at[r], s, c1, r1).wait_send())

    def sent_out(s1, r1, k, src, me):
        pl.when(jnp.logical_not(me))(
            lambda: remote(src, obuf.at[slot], os.at[k], orr.at[slot], s1, c2, r1).wait_send())

    each(sent_main)
    each(sent_edge)
    each(sent_mask)
    outgoing(sent_out)
    for k in range(1, n_src):
        pz(k).wait_send()
        wz(k).wait_send()
        share_copy(k).wait_send()


def by_pixel(
    features, layout, conv_weight, conv_bias, head_weight, transmission, point_weight, assignment
):
    n_src, n_chan, n_row = (lax.axis_size(a) for a in ("src", "chan", "row"))
    s = lax.axis_index("src")
    layers = conv_weight.shape[1]
    part, strip, block = features.shape
    ch = part * n_chan
    width = block * n_src
    rows = strip * n_row
    own = block // (n_chan * n_row)
    lanes = 2 * ch
    span = 2**layers
    pairs = features.reshape(part, strip // 2, 2, block // 2, 2).transpose(3, 1, 4, 2, 0)
    pairs = pairs.reshape(block // 2, strip // 2, lanes)
    w = conv_weight[0].reshape(layers, 3, 3, ch, ch).transpose(0, 2, 1, 3, 4)
    zero = jnp.zeros((layers, ch, ch), w.dtype)
    packed = [jnp.concatenate([w[:, 1, b], w[:, 0, b]], -1) for b in range(3)]
    packed.append(jnp.concatenate([w[:, 2, 0], w[:, 2, 1]], -1))
    packed.append(jnp.concatenate([w[:, 2, 2], zero], -1))
    packed = jnp.stack(packed, 1).reshape(2, layers // 2 * 5, ch, lanes)
    planes2 = head_weight.shape[2]
    half_tile = layout.shape[1] // block
    mask = lax.dynamic_slice_in_dim(layout, (s % half_tile) * block, block, 1).astype(jnp.float32)
    mask = mask.reshape(strip // 8, 8, 4, own // span, 2, span // 2).transpose(2, 0, 4, 1, 3, 5)
    mask = mask.reshape(4, strip // 4, 4 * own)
    spec = lambda shape, kind=jnp.bfloat16: pltpu.VMEM(shape, kind)
    scratch = []
    slots = block // 4
    segs = rows // span
    scratch.append(spec((span + 2, slots * segs, 2 * lanes)))
    for _ in range(2):
        for l in range(1, layers):
            scratch.append(spec((span + 2 * 2**l, (slots - 2 * 2**l) * segs, 2 * lanes)))
        scratch.append(spec((span * (slots - span) * segs, lanes), jnp.float32))
    groups = rows // 8
    scratch += [
        spec((4, slots, strip // 2, lanes)),
        spec((n_src,) + packed.shape),
        spec((n_src, planes2 + (layers + 7) // 8 * 8, lanes), jnp.float32),
        spec((2,) + mask.shape[1:], jnp.float32),
        spec((n_src, layers, 16 * ch, 2 * lanes)),
        spec((groups, planes2, lanes), jnp.float32),
        spec((groups, planes2 // 2, 8 * own), jnp.float32),
        spec((2 * n_src, planes2 // 2, 8 * own), jnp.float32),
        spec((4, slots * strip // 2, lanes), jnp.float32),
        spec((span * slots * segs + 16, lanes), jnp.float32),
    ]
    dma = pltpu.SemaphoreType.DMA
    for count in (4, 4, 4, 4, n_src, n_src, n_src, n_src, n_src, n_src, 4, 2, 2 * n_src, 2 * n_src):
        scratch.append(dma((count,)))
    scratch += [dma(())]
    vmem = pl.BlockSpec(memory_space=pltpu.VMEM)
    out = pl.pallas_call(
        functools.partial(pixel_kernel, layers, n_src),
        out_shape=jax.ShapeDtypeStruct((planes2 // 2, 8, width // n_chan), jnp.float32),
        in_specs=[vmem] * 8,
        out_specs=vmem,
        scratch_shapes=scratch,
        compiler_params=pltpu.CompilerParams(
            vmem_limit_bytes=56 * 2**20, collective_id=0, has_side_effects=True),
    )(pairs, packed, head_weight[0].T, transmission, conv_bias[0], mask, point_weight[None], assignment.reshape(1, -1))
    return out[:, None]


def solution(mesh):
    in_specs = (
        P("chan", ("grp", "row"), "src"),
        P(("grp", "row"), "chan"),
        P("src", None, None, None, None),
        P("src", None, None),
        P("src", None, None),
        P("src", None),
        P(),
        P(),
    )
    out_specs = P(None, ("grp", "row"), "src", "chan")

    def shards(*args):
        features, weights = args[0], args[2]
        halo = 2 ** weights.shape[1] - 1
        own = features.shape[2] // (mesh.shape["chan"] * mesh.shape["row"])
        fits = own >= 2 * halo and mesh.shape["chan"] == mesh.shape["row"] == 2
        body = by_pixel if fits and mesh.shape["src"] == 4 else by_cluster
        return body(*args)

    return jax.shard_map(shards, mesh=mesh, in_specs=in_specs, out_specs=out_specs, check_vma=False)
```

```python
import functools
import math

import jax
import jax.numpy as jnp
from jax import lax
from jax.experimental import pallas as pl
from jax.experimental.pallas import tpu as pltpu
from jax.sharding import PartitionSpec as P


def with_halo(block, sides, width):
    for axis, dim in sides:
        count = lax.axis_size(axis)
        forward = [(i, i + 1) for i in range(count - 1)]
        backward = [(target, source) for source, target in forward]
        low = lax.ppermute(
            lax.slice_in_dim(block, block.shape[dim] - width, None, axis=dim), axis, forward
        )
        high = lax.ppermute(lax.slice_in_dim(block, 0, width, axis=dim), axis, backward)
        block = jnp.concatenate([low, block, high], axis=dim)
    return block


def advance(core_cells, padded, weights, biases, dilation):
    tile_rows, tile_cols = (core_cells.shape[1], core_cells.shape[2])
    kernel = weights.reshape(3, 3, weights.shape[1], weights.shape[2])
    window = padded[:, : tile_rows + 2 * dilation, : tile_cols + 2 * dilation]
    summed = lax.conv_general_dilated(
        window[None],
        kernel,
        (1, 1),
        "VALID",
        rhs_dilation=(dilation, dilation),
        dimension_numbers=("NCHW", "HWIO", "NCHW"),
        preferred_element_type=jnp.float32,
    )[0]
    summed = summed + biases[:, None, None]
    return (core_cells.astype(jnp.float32) + jax.nn.gelu(summed, approximate=True)).astype(
        jnp.bfloat16
    )


def by_cluster(
    features, layout, conv_weight, conv_bias, head_weight, transmission, point_weight, assignment
):
    channels = lax.all_gather(features, "chan", axis=0, tiled=True)
    full_cache = lax.all_gather(channels, "src", axis=2, tiled=True)
    column_width = full_cache.shape[2] // lax.axis_size("chan")
    tile_cache = lax.dynamic_slice_in_dim(
        full_cache, lax.axis_index("chan") * column_width, column_width, 2
    )
    weights = conv_weight[0]
    biases = conv_bias[0]
    hidden = tile_cache
    for layer_index in range(weights.shape[0]):
        dilation = 2**layer_index
        padded = with_halo(hidden, (("chan", 2), ("row", 1)), dilation)
        hidden = advance(hidden, padded, weights[layer_index], biases[layer_index], dilation)
    field_map = jnp.einsum(
        "ihw,ik->khw", hidden, head_weight[0], preferred_element_type=jnp.float32
    )
    field_map = field_map + layout.astype(jnp.float32)[None] * transmission[0][:, None, None]
    planes = field_map.shape[0] // 2
    power_map = field_map[:planes] ** 2 + field_map[planes:] ** 2
    chosen = assignment[:, 0] == lax.axis_index("src")
    cluster_share = jnp.sum(jnp.where(chosen, point_weight, jnp.zeros((), jnp.float32))) / jnp.sum(
        point_weight
    )
    summed = lax.psum_scatter(
        (power_map * cluster_share).astype(jnp.bfloat16), "src", scatter_dimension=1, tiled=True
    ).astype(jnp.float32)
    return summed[:, None]


def gelu_of_half(v):
    c = 2.0 * math.sqrt(2.0 / math.pi)
    return v + v * jnp.tanh(v * (c + (c * 4.0 * 0.044715) * (v * v)))


def half_lanes(shape):
    return lax.broadcasted_iota(jnp.int32, shape, len(shape) - 1) < shape[-1] // 2


def pair_up(h, d, segs):
    n, sub, lanes = h.shape
    low = half_lanes((1, sub, lanes))
    if d * segs < sub:
        first = lax.broadcasted_iota(jnp.int32, (1, sub, lanes), 1) < sub // 2
        other = pltpu.roll(pltpu.roll(h, sub // 2, 1), lanes // 2, 2)
        return jnp.where(first == low, h, other)
    g = d * segs // sub
    turned = pltpu.roll(h, lanes // 2, 2)
    groups = n // g
    at = lambda x, m: x[m * g : (m + 1) * g]
    out = []
    for i in range((groups + 2) // 2):
        u, v = 2 * i - 1, 2 * i
        if i == 0:
            out += [at(turned, v), at(h, v)]
        elif v == groups:
            out += [at(h, u), at(turned, u)]
        else:
            out += [jnp.where(low, at(h, u), at(turned, v)), jnp.where(low, at(turned, u), at(h, v))]
    return jnp.concatenate(out, axis=0)


def shift_segment(h, segs, down):
    sub = lax.broadcasted_iota(jnp.int32, (1,) + h.shape[1:], 1) % segs
    if down:
        return jnp.where(sub == 0, 0.0, pltpu.roll(h, 1, 1))
    return jnp.where(sub == segs - 1, 0.0, pltpu.roll(h, h.shape[1] - 1, 1))


MESH = pl.DeviceIdType.MESH
CHUNKS = 2


def xor(s, k):
    total = s
    bit = 1
    while bit <= k:
        if k & bit:
            total = total + bit - 2 * bit * ((s // bit) % 2)
        bit *= 2
    return total


def pixel_kernel(
    layers, n_src, f_ref, w_ref, h_ref, tr_ref, b_ref, y_ref, pw_ref, as_ref, o_ref, *scratch
):
    first, bufs = scratch[0], (scratch[1 : layers + 1], scratch[layers + 1 : 2 * layers + 1])
    got, wraw, pbuf, mbuf, wide, acc, sbuf, obuf, stage, rowbuf, t_ref, m_ref = scratch[2 * layers + 1 : 2 * layers + 13]
    fs, fr, es, er, ws, wr, ys, yr, vs, vr, ps, pr, ms, mr, os, orr = scratch[2 * layers + 13 :]
    gp, s, c, r = (lax.axis_index(a) for a in ("grp", "src", "chan", "row"))
    lanes = t_ref.shape[2]
    half_rows = t_ref.shape[1]
    rows = 4 * half_rows
    piece = t_ref.shape[0] // 8
    here = 2 * c + r
    side = c

    barrier = pltpu.get_barrier_semaphore()
    for s1 in range(n_src):
        for c1 in range(2):
            for r1 in range(2):
                @pl.when(jnp.logical_not((s == s1) & (c == c1) & (r == r1)))
                def _():
                    pl.semaphore_signal(
                        barrier, inc=1, device_id={"src": s1, "chan": c1, "row": r1},
                        device_id_type=MESH,
                    )
    pl.semaphore_signal(barrier, inc=1, device_id={"grp": 1 - gp}, device_id_type=MESH)
    ch = lanes // 2
    planes2 = h_ref.shape[0]
    ia = lax.broadcasted_iota(jnp.int32, (planes2, planes2), 0)
    ib = lax.broadcasted_iota(jnp.int32, (planes2, planes2), 1)
    column = jnp.sum(jnp.where(ia == ib, tr_ref[...], 0.0), axis=1, keepdims=True)
    pbuf[0, :planes2, :] = jnp.concatenate(
        [h_ref[...].astype(jnp.float32), jnp.broadcast_to(column, (planes2, ch))], axis=1)
    bias_half = 0.5 * b_ref[...]
    pbuf[0, planes2 : planes2 + layers, :] = jnp.concatenate([bias_half, bias_half], axis=1)

    part, strip, block = f_ref.shape
    for ci in range(part):
        rowbuf[ci * strip : (ci + 1) * strip, :] = f_ref[ci].astype(jnp.float32)
    kin = lax.broadcasted_iota(jnp.int32, (block // 2, 2 * block), 1)
    kout = lax.broadcasted_iota(jnp.int32, (block // 2, 2 * block), 0)
    pick = jnp.where(kin % block == 2 * kout + kin // block, 1.0, 0.0).astype(jnp.bfloat16)
    blank = jnp.zeros((2 * part, block), jnp.bfloat16)
    base = part * strip
    for y4 in range(strip // 4):
        cells = []
        for y2 in (2 * y4, 2 * y4 + 1):
            both_rows = jnp.concatenate(
                [rowbuf[pl.ds(2 * y2 + yp, part, stride=strip), :] for yp in range(2)], axis=0
            ).astype(jnp.bfloat16)
            cells.append(jnp.concatenate([both_rows, blank], axis=1))
            cells.append(jnp.concatenate([blank, both_rows], axis=1))
        moved = lax.dot_general(
            pick, jnp.concatenate(cells, axis=0), (((1,), (1,)), ((), ())),
            preferred_element_type=jnp.float32)
        for e in range(2):
            rowbuf[pl.ds(base + 2 * y4 + e, block // 2, stride=half_rows), :] = moved[
                :, e * lanes : (e + 1) * lanes]
    for x8 in range(block // 16):
        t_ref[8 * x8 : 8 * x8 + 8] = rowbuf[
            base + 8 * x8 * half_rows : base + 8 * (x8 + 1) * half_rows, :
        ].reshape(8, half_rows, lanes).astype(t_ref.dtype)

    per = layers // 2
    for l in range(layers):
        for i, (one, two) in enumerate(((1, 0), (4, 3), (7, 6), (2, 5), (8, None))):
            other = jnp.zeros((ch, ch), w_ref.dtype) if two is None else w_ref[l, two]
            wraw[0, l // per, (l % per) * 5 + i] = jnp.concatenate([w_ref[l, one], other], axis=1)

    pl.semaphore_wait(barrier, 4 * n_src)

    def remote(src, dst, a, b, s1, c1, r1):
        return pltpu.make_async_remote_copy(
            src_ref=src, dst_ref=dst, send_sem=a, recv_sem=b,
            device_id={"src": s1, "chan": c1, "row": r1}, device_id_type=MESH,
        )

    def main_copy(c1, r1):
        return (
            t_ref.at[pl.ds(piece * (3 * c1 + 2 * r1), 3 * piece)],
            got.at[here, pl.ds(piece * (1 - c1), 3 * piece)],
        )

    def edge_copy(c1, r1):
        at = 7 * (1 - c1) if c1 == r1 else 1 + 5 * c1
        return t_ref.at[pl.ds(piece * at, piece)], got.at[here, pl.ds(piece * 3 * c1, piece)]

    def each(act):
        for c1 in (0, 1):
            for r1 in (0, 1):
                k = 2 * c1 + r1
                me = (c == c1) & (r == r1)
                act(c1, r1, k, me)

    def send_main(c1, r1, k, me):
        src, dst = main_copy(c1, r1)
        pl.when(jnp.logical_not(me))(
            lambda: remote(src, dst, fs.at[k], fr.at[here], s, c1, r1).start())
        pl.when(me)(lambda: pltpu.make_async_copy(src, dst, fr.at[here]).start())

    def edge_step(c1):
        return 1 - 2 * c1

    def send_edge(c1, r1, k, me):
        src, dst = edge_copy(c1, r1)
        if c1 == r1:
            s1 = s + edge_step(c1)
            pl.when((s1 >= 0) & (s1 < n_src))(
                lambda: remote(src, dst, es.at[k], er.at[here], s1, c1, r1).start())
        else:
            pl.when(jnp.logical_not(me))(
                lambda: remote(src, dst, es.at[k], er.at[here], s, c1, r1).start())
            pl.when(me)(lambda: pltpu.make_async_copy(src, dst, er.at[here]).start())

    def send_mask(c1, r1, k, me):
        src, dst = m_ref.at[k], mbuf.at[r]
        owner = c == (2 * s) // n_src
        pl.when(owner & jnp.logical_not(me))(
            lambda: remote(src, dst, ms.at[k], mr.at[r], s, c1, r1).start())
        pl.when(owner & me)(lambda: pltpu.make_async_copy(src, dst, mr.at[r]).start())

    each(send_main)
    each(send_edge)

    blocks = wraw.shape[2] // 2

    def wz(k):
        at = pl.ds(gp * blocks, blocks)
        return remote(wraw.at[0, r, at], wraw.at[k, r, at], ws.at[k], wr.at[k], xor(s, k), c, r)

    def wy(k, g1):
        piece_of = wraw.at[k, r, pl.ds(g1 * blocks, blocks)]
        return pltpu.make_async_remote_copy(
            src_ref=piece_of, dst_ref=piece_of, send_sem=ys.at[k], recv_sem=yr.at[k],
            device_id={"grp": 1 - gp}, device_id_type=MESH,
        )

    def pz(k):
        return remote(pbuf.at[0], pbuf.at[k], ps.at[k], pr.at[k], xor(s, k), c, r)

    for k in range(1, n_src):
        pz(k).start()
        wz(k).start()
    column = pl.multiple_of((s % (y_ref.shape[1] // block)) * block, block)
    wanted = y_ref[:, pl.ds(column, block)].astype(jnp.bfloat16)
    unit = half_rows // 2
    xin = lax.broadcasted_iota(jnp.int32, (block, block), 0)
    xout = lax.broadcasted_iota(jnp.int32, (block, block), 1)
    from_x = xout // (4 * unit) * (4 * unit) + (xout // unit % 2) * 2 * unit + (xout // (2 * unit) % 2) * unit + xout % unit
    sorted_x = jnp.dot(
        wanted, jnp.where(xin == from_x, 1.0, 0.0).astype(jnp.bfloat16), preferred_element_type=jnp.float32)
    seg_of = lax.broadcasted_iota(jnp.int32, (8, block), 1) // (block // 8)
    sub_of = lax.broadcasted_iota(jnp.int32, (8, block), 0)
    for g in range(strip // 8):
        tile = sorted_x[8 * g : 8 * g + 8]
        turned = tile
        for e in range(1, 8):
            moved = pltpu.roll(pltpu.roll(tile, 8 - e, 0), e * block // 8, 1)
            turned = jnp.where((seg_of - sub_of + 8) % 8 == e, moved, turned)
        for kt in range(4):
            m_ref[kt, 2 * g : 2 * g + 2, :] = turned[2 * kt : 2 * kt + 2]
    each(send_mask)

    for k in range(n_src):
        for l in range(layers):
            for at, cut in ((0, lanes), (12 * ch, 0)):
                wide[k, l, at : at + 4 * ch, cut : cut + lanes] = jnp.zeros((4 * ch, lanes), wide.dtype)
    outside = ((here == 0) & (s == 0)) | ((here == 3) & (s == n_src - 1))

    @pl.when(outside)
    def _():
        for k in range(4):
            got[k, pl.ds(piece * 3 * side, piece)] = jnp.zeros((piece,) + got.shape[2:], got.dtype)

    def build(k):
        low = lax.broadcasted_iota(jnp.int32, (ch, lanes), 1) < ch
        per = layers // 2
        for l in range(layers):
            raw = lambda i: wraw[k, l // per, (l % per) * 5 + i].astype(jnp.float32) * 0.5
            firsts = [raw(b) for b in range(3)]
            q0, q1 = raw(3), raw(4)
            seconds = [q0, pltpu.roll(q0, ch, 1), q1]
            for b in range(3):
                w10, w2 = firsts[b], seconds[b]
                swap = pltpu.roll(w10, ch, 1)
                blocks = [
                    w10,
                    jnp.where(low, w2, swap),
                    jnp.where(low, 0.0, pltpu.roll(w2, ch, 1)),
                    jnp.where(low, swap, 0.0),
                ]
                for j in range(4):
                    v = blocks[j].astype(wide.dtype)
                    for ic in range(2):
                        at = (b + ic) * 4 * ch + j * ch
                        wide[k, l, at : at + ch, ic * lanes : (ic + 1) * lanes] = v

    build(0)

    def wait_main(c1, r1, k, me):
        src, _ = main_copy(0, 0)
        dst = got.at[k, pl.ds(piece * (1 - side), 3 * piece)]
        pl.when(jnp.logical_not(me))(
            lambda: remote(src, dst, fs.at[k], fr.at[k], s, c1, r1).wait_recv())
        pl.when(me)(lambda: pltpu.make_async_copy(src, dst, fr.at[k]).wait())

    def wait_edge(c1, r1, k, me):
        src, _ = edge_copy(0, 0)
        dst = got.at[k, pl.ds(piece * 3 * side, piece)]
        far = c == r
        inside = jnp.logical_not(outside)
        pl.when(jnp.where(far, inside, jnp.logical_not(me)))(
            lambda: remote(src, dst, es.at[k], er.at[k], s, c1, r1).wait_recv())
        pl.when(jnp.logical_not(far) & me)(
            lambda: pltpu.make_async_copy(src, dst, er.at[k]).wait())

    def take(k):
        wz(k).wait_recv()
        wy(k, gp).start()

    take(1)
    each(wait_main)
    each(wait_edge)
    q = ch // 2
    span = 2**layers
    segs = rows // span
    slots = got.shape[1]
    own_cols = 2 * slots - 2 * span
    rin = lax.broadcasted_iota(jnp.int32, (2 * lanes, 2 * lanes), 0)
    rout = lax.broadcasted_iota(jnp.int32, (2 * lanes, 2 * lanes), 1)
    want = (rout // q % 2) * lanes + (rout // ch % 2) * ch + (rout // lanes) * q + rout % q
    place = jnp.where(rin == want, 1.0, 0.0).astype(t_ref.dtype)
    for r1 in range(2):
        lhs = jnp.concatenate(
            [got[2 * c1 + r1].reshape(slots * half_rows, lanes) for c1 in range(2)], axis=1)
        v = jnp.dot(lhs, place, preferred_element_type=jnp.float32)
        for yp in range(2):
            stage[2 * r1 + yp] = v[:, yp * lanes : (yp + 1) * lanes]
    mrows = slots * segs
    rowbuf[0:8, :] = jnp.zeros((8, lanes), jnp.float32)
    rowbuf[8 + span * mrows : 16 + span * mrows, :] = jnp.zeros((8, lanes), jnp.float32)
    for r1 in range(2):
        for y2 in range(half_rows):
            for yp in range(2):
                y = 2 * y2 + yp
                at = 8 + (y % span) * mrows + r1 * (segs // 2) + y // span
                rowbuf[pl.ds(at, slots, stride=segs), :] = stage[
                    2 * r1 + yp, pl.ds(y2, slots, stride=half_rows), :]
    low_lanes = half_lanes((1, 8, lanes))
    as_tiles = lambda v: v.reshape(-1, 8, lanes)
    for y in range(span):
        at = 8 + y * mrows
        own = as_tiles(rowbuf[at : at + mrows, :])
        near = jnp.where(
            low_lanes, as_tiles(rowbuf[at + segs : at + segs + mrows, :]),
            as_tiles(rowbuf[at - segs : at - segs + mrows, :]))
        places = [(y, own, near)]
        if y == span - 1:
            places.append((-1, shift_segment(own, segs, True), shift_segment(near, segs, True)))
        if y == 0:
            places.append((span, shift_segment(own, segs, False), shift_segment(near, segs, False)))
        for yy, a, b in places:
            first[yy + 1, :, :lanes] = a.reshape(mrows, lanes).astype(first.dtype)
            first[yy + 1, :, lanes:] = b.reshape(mrows, lanes).astype(first.dtype)

    at_left = (here == 0) & (s == 0)
    at_right = (here == 3) & (s == n_src - 1)
    for r1 in range(2):
        for_self = (c == (2 * s) // n_src) & (r == r1)
        pl.when(jnp.logical_not(for_self))(
            lambda: remote(m_ref.at[0], mbuf.at[r1], ms.at[0], mr.at[r1], s, c, r).wait_recv())
        pl.when(for_self)(
            lambda: pltpu.make_async_copy(m_ref.at[0], mbuf.at[r1], mr.at[r1]).wait())

    def share_copy(k):
        return remote(wraw.at[k, r], wraw.at[k, r], vs.at[k], vr.at[k], s, c, 1 - r)

    total = jnp.sum(pw_ref[...], axis=1, keepdims=True)

    def store_next(dst, h, y, d):
        wider = 2 * d
        places = [(y, h)]
        if y >= span - wider:
            places.append((y - span, shift_segment(h, segs, True)))
        if y < wider:
            places.append((y + span, shift_segment(h, segs, False)))
        for yy, v in places:
            v = pair_up(v, d, segs)
            n = v.shape[0]
            out = (slots // 2 - own_cols // 4) * segs // 8
            v = jnp.concatenate(
                [jnp.where(at_left, 0.0, v[:out]), v[out : n - out], jnp.where(at_right, 0.0, v[n - out :])],
                axis=0)
            g = wider * segs // 8
            near = jnp.where(low_lanes, v[2 * g :], v[: n - 2 * g])
            own = v[g : n - g]
            dst[yy + wider, :, :lanes] = own.reshape(-1, lanes).astype(dst.dtype)
            dst[yy + wider, :, lanes:] = near.reshape(-1, lanes).astype(dst.dtype)

    def multiply(k, l, ys):
        d = 2**l
        src = first if l == 0 else bufs[k % 2][l - 1]
        lhs = jnp.concatenate(
            [jnp.concatenate([src[y + j * d] for y in ys], axis=0) for j in range(4)], axis=1)
        return jnp.dot(lhs, wide[k, l], preferred_element_type=jnp.float32)

    def activate(k, l, ys, out):
        d = 2**l
        src = first if l == 0 else bufs[k % 2][l - 1]
        dst = bufs[k % 2][l]
        n = src.shape[1]
        bias = pbuf[k, 2 * q2 + l : 2 * q2 + l + 1, :]
        for i, y in enumerate(ys):
            for e in range(2):
                z = out[i * n : (i + 1) * n, e * lanes : (e + 1) * lanes] + bias
                yy = y + e * d
                h = src[yy + d, :, :lanes].astype(jnp.float32) + gelu_of_half(z)
                if l + 1 < layers:
                    store_next(dst, h.reshape(-1, 8, lanes), yy, d)
                else:
                    dst[yy * n : (yy + 1) * n, :] = h

    def finish(k, cid):
        share = jnp.sum(jnp.where(as_ref[...] == cid, pw_ref[...], 0.0), axis=1, keepdims=True) / total
        final = bufs[k % 2][layers - 1]
        n = final.shape[0] // span
        head = pbuf[k, : 2 * q2, :]
        low = lax.broadcasted_iota(jnp.int32, head.shape, 1) < ch
        h_lo = jnp.where(low, head, 0.0)
        h_hi = jnp.where(low, 0.0, pltpu.roll(head, ch, 1))
        tcol = head[:, ch : ch + 1]
        hw = jnp.concatenate([h_lo[:q2], h_hi[:q2], h_lo[q2:], h_hi[q2:]], axis=0).astype(jnp.bfloat16)
        tr = jnp.concatenate([tcol[:q2], tcol[:q2], tcol[q2:], tcol[q2:]], axis=0)
        per = rows // 16
        for g in range(rows // 8):
            at = 8 * (g % 2) * n + g // 2
            block = jnp.concatenate(
                [final[pl.ds(at + b * n, n // segs, stride=segs), :] for b in range(8)], axis=0
            ).astype(jnp.bfloat16)
            field = lax.dot_general(
                hw, block, (((1,), (1,)), ((), ())), preferred_element_type=jnp.float32)
            m = mbuf[g // per, 2 * (g % per) : 2 * (g % per) + 2]
            mm = jnp.concatenate(
                [jnp.broadcast_to(m[i : i + 1], (q2, m.shape[1])) for i in (0, 1, 0, 1)], axis=0)
            field = field + mm * tr
            power = (field[: 2 * q2] ** 2 + field[2 * q2 :] ** 2) * share
            if k == 0:
                acc[g] = power
            else:
                acc[g] = acc[g] + power

    q2 = h_ref.shape[0] // 2

    def cross(k):
        wy(k, 1 - gp).wait_recv()
        share_copy(k).start()

    def receive(k):
        remote(
            wraw.at[k, 1 - r], wraw.at[k, 1 - r], vs.at[k], vr.at[k], s, c, 1 - r
        ).wait_recv()
        pz(k).wait_recv()
        build(k)

    tops = lambda d: [y for y in range(span) if y % (2 * d) < d]
    ahead = layers // 2
    cross(1)
    take(2)
    pending = None
    for step in range(ahead * (n_src + 1)):
        k0, l0 = step // ahead, step % ahead
        if l0 == 0 and 0 < k0 < n_src:
            receive(k0)
        if l0 == 0 and k0 + 1 < n_src and k0:
            cross(k0 + 1)
            if k0 + 2 < n_src:
                take(k0 + 2)
        for k, l in ((k0, l0), (k0 - 1, l0 + ahead)):
            if not 0 <= k < n_src:
                continue
            ys_all = tops(2**l)
            count = len(ys_all) // CHUNKS
            for i in range(CHUNKS):
                some = ys_all[i * count : (i + 1) * count]
                if pending and pending[0] == k and pending[1] != l:
                    activate(*pending)
                    pending = None
                out = multiply(k, l, some)
                if pending:
                    activate(*pending)
                pending = (k, l, some, out)
        if l0 == ahead - 1 and k0:
            if pending[0] == k0 - 1:
                activate(*pending)
                pending = None
            finish(k0 - 1, xor(s, k0 - 1))

    pin = lax.broadcasted_iota(jnp.int32, (2 * lanes, 2 * lanes), 0)
    pout = lax.broadcasted_iota(jnp.int32, (2 * lanes, 2 * lanes), 1)
    column = pout % own_cols
    half = span // 2
    source = (
        (column // half % 2) * lanes + pout // own_cols * (own_cols // 2)
        + column // span * half + column % half)
    order = jnp.where(pin == source, 1.0, 0.0).astype(jnp.bfloat16)
    both = jnp.concatenate(
        [jnp.concatenate([acc[g, :q2], acc[g, q2:]], axis=1) for g in range(rows // 8)], axis=0)
    sbuf[...] = jnp.dot(
        both.astype(jnp.bfloat16), order, preferred_element_type=jnp.float32
    ).reshape(sbuf.shape)

    c2 = (2 * s) // n_src
    slot = 4 * (s % 2) + here

    def outgoing(act):
        for s1 in range(n_src):
            for r1 in range(2):
                k = 2 * s1 + r1
                src = sbuf.at[n_src * r1 + s1]
                me = (s == s1) & (c == c2) & (r == r1)
                act(s1, r1, k, src, me)

    def send_out(s1, r1, k, src, me):
        dst = obuf.at[slot]
        pl.when(jnp.logical_not(me))(
            lambda: remote(src, dst, os.at[k], orr.at[slot], s1, c2, r1).start())
        pl.when(me)(lambda: pltpu.make_async_copy(src, dst, orr.at[slot]).start())

    outgoing(send_out)
    mine = c == c2
    for k in range(2 * n_src):
        me = mine & (slot == k)
        src = sbuf.at[0]
        pl.when(jnp.logical_not(me))(
            lambda: remote(src, obuf.at[k], os.at[k], orr.at[k], s, c, r).wait_recv())
        pl.when(me)(lambda: pltpu.make_async_copy(src, obuf.at[k], orr.at[k]).wait())
    for b in range(8):
        o_ref[:, b, :] = jnp.concatenate(
            [obuf[k, :, b * own_cols : (b + 1) * own_cols] for k in range(2 * n_src)], axis=1)

    def sent_main(c1, r1, k, me):
        src, dst = main_copy(c1, r1)
        pl.when(jnp.logical_not(me))(
            lambda: remote(src, dst, fs.at[k], fr.at[here], s, c1, r1).wait_send())

    def sent_edge(c1, r1, k, me):
        src, dst = edge_copy(c1, r1)
        s1 = s + edge_step(c1)
        gone = (s1 >= 0) & (s1 < n_src) if c1 == r1 else jnp.logical_not(me)
        pl.when(gone)(lambda: remote(src, dst, es.at[k], er.at[here], s, c1, r1).wait_send())

    def sent_mask(c1, r1, k, me):
        owner = c == (2 * s) // n_src
        pl.when(owner & jnp.logical_not(me))(
            lambda: remote(m_ref.at[k], mbuf.at[r], ms.at[k], mr.at[r], s, c1, r1).wait_send())

    def sent_out(s1, r1, k, src, me):
        pl.when(jnp.logical_not(me))(
            lambda: remote(src, obuf.at[slot], os.at[k], orr.at[slot], s1, c2, r1).wait_send())

    each(sent_main)
    each(sent_edge)
    each(sent_mask)
    outgoing(sent_out)
    for k in range(1, n_src):
        pz(k).wait_send()
        wz(k).wait_send()
        wy(k, gp).wait_send()
        share_copy(k).wait_send()


def by_pixel(
    features, layout, conv_weight, conv_bias, head_weight, transmission, point_weight, assignment
):
    n_src, n_chan, n_row = (lax.axis_size(a) for a in ("src", "chan", "row"))
    layers = conv_weight.shape[1]
    part, strip, block = features.shape
    ch = part * n_chan
    width = block * n_src
    rows = strip * n_row
    own = block // (n_chan * n_row)
    lanes = 2 * ch
    span = 2**layers
    planes2 = head_weight.shape[2]
    spec = lambda shape, kind=jnp.bfloat16: pltpu.VMEM(shape, kind)
    scratch = []
    slots = block // 4
    segs = rows // span
    scratch.append(spec((span + 2, slots * segs, 2 * lanes)))
    for _ in range(2):
        for l in range(1, layers):
            scratch.append(spec((span + 2 * 2**l, (slots - 2 * 2**l) * segs, 2 * lanes)))
        scratch.append(spec((span * (slots - span) * segs, lanes), jnp.float32))
    groups = rows // 8
    scratch += [
        spec((4, slots, strip // 2, lanes)),
        spec((n_src, 2, layers // 2 * 5, ch, lanes)),
        spec((n_src, planes2 + (layers + 7) // 8 * 8, lanes), jnp.float32),
        spec((2, strip // 4, block), jnp.float32),
        spec((n_src, layers, 16 * ch, 2 * lanes)),
        spec((groups, planes2, lanes), jnp.float32),
        spec((groups, planes2 // 2, 8 * own), jnp.float32),
        spec((2 * n_src, planes2 // 2, 8 * own), jnp.float32),
        spec((4, slots * strip // 2, lanes), jnp.float32),
        spec((span * slots * segs + 16, lanes), jnp.float32),
        spec((block // 2, strip // 2, lanes)),
        spec((4, strip // 4, block), jnp.float32),
    ]
    dma = pltpu.SemaphoreType.DMA
    for count in (4, 4, 4, 4, n_src, n_src, n_src, n_src, n_src, n_src, n_src, n_src, 4, 2, 2 * n_src, 2 * n_src):
        scratch.append(dma((count,)))
    vmem = pl.BlockSpec(memory_space=pltpu.VMEM)
    out = pl.pallas_call(
        functools.partial(pixel_kernel, layers, n_src),
        out_shape=jax.ShapeDtypeStruct((planes2 // 2, 8, width // n_chan), jnp.float32),
        in_specs=[vmem] * 8,
        out_specs=vmem,
        scratch_shapes=scratch,
        compiler_params=pltpu.CompilerParams(
            vmem_limit_bytes=26 * 2**20, collective_id=0, has_side_effects=True),
    )(features, conv_weight[0], head_weight[0].T, transmission, conv_bias[0], layout, point_weight[None], assignment.reshape(1, -1))
    return out[:, None]


def solution(mesh):
    in_specs = (
        P("chan", ("grp", "row"), "src"),
        P(("grp", "row"), "chan"),
        P("src", None, None, None, None),
        P("src", None, None),
        P("src", None, None),
        P("src", None),
        P(),
        P(),
    )
    out_specs = P(None, ("grp", "row"), "src", "chan")

    def shards(*args):
        features, weights = args[0], args[2]
        halo = 2 ** weights.shape[1] - 1
        own = features.shape[2] // (mesh.shape["chan"] * mesh.shape["row"])
        fits = own >= 2 * halo and mesh.shape["chan"] == mesh.shape["row"] == 2
        body = by_pixel if fits and mesh.shape["src"] == 4 and mesh.shape["grp"] == 2 else by_cluster
        return body(*args)

    return jax.shard_map(shards, mesh=mesh, in_specs=in_specs, out_specs=out_specs, check_vma=False)
```

```python
import functools
import math

import jax
import jax.numpy as jnp
from jax import lax
from jax.experimental import pallas as pl
from jax.experimental.pallas import tpu as pltpu
from jax.sharding import PartitionSpec as P


def with_halo(block, sides, width):
    for axis, dim in sides:
        count = lax.axis_size(axis)
        forward = [(i, i + 1) for i in range(count - 1)]
        backward = [(target, source) for source, target in forward]
        low = lax.ppermute(
            lax.slice_in_dim(block, block.shape[dim] - width, None, axis=dim), axis, forward
        )
        high = lax.ppermute(lax.slice_in_dim(block, 0, width, axis=dim), axis, backward)
        block = jnp.concatenate([low, block, high], axis=dim)
    return block


def advance(core_cells, padded, weights, biases, dilation):
    tile_rows, tile_cols = (core_cells.shape[1], core_cells.shape[2])
    kernel = weights.reshape(3, 3, weights.shape[1], weights.shape[2])
    window = padded[:, : tile_rows + 2 * dilation, : tile_cols + 2 * dilation]
    summed = lax.conv_general_dilated(
        window[None],
        kernel,
        (1, 1),
        "VALID",
        rhs_dilation=(dilation, dilation),
        dimension_numbers=("NCHW", "HWIO", "NCHW"),
        preferred_element_type=jnp.float32,
    )[0]
    summed = summed + biases[:, None, None]
    return (core_cells.astype(jnp.float32) + jax.nn.gelu(summed, approximate=True)).astype(
        jnp.bfloat16
    )


def by_cluster(
    features, layout, conv_weight, conv_bias, head_weight, transmission, point_weight, assignment
):
    channels = lax.all_gather(features, "chan", axis=0, tiled=True)
    full_cache = lax.all_gather(channels, "src", axis=2, tiled=True)
    column_width = full_cache.shape[2] // lax.axis_size("chan")
    tile_cache = lax.dynamic_slice_in_dim(
        full_cache, lax.axis_index("chan") * column_width, column_width, 2
    )
    weights = conv_weight[0]
    biases = conv_bias[0]
    hidden = tile_cache
    for layer_index in range(weights.shape[0]):
        dilation = 2**layer_index
        padded = with_halo(hidden, (("chan", 2), ("row", 1)), dilation)
        hidden = advance(hidden, padded, weights[layer_index], biases[layer_index], dilation)
    field_map = jnp.einsum(
        "ihw,ik->khw", hidden, head_weight[0], preferred_element_type=jnp.float32
    )
    field_map = field_map + layout.astype(jnp.float32)[None] * transmission[0][:, None, None]
    planes = field_map.shape[0] // 2
    power_map = field_map[:planes] ** 2 + field_map[planes:] ** 2
    chosen = assignment[:, 0] == lax.axis_index("src")
    cluster_share = jnp.sum(jnp.where(chosen, point_weight, jnp.zeros((), jnp.float32))) / jnp.sum(
        point_weight
    )
    summed = lax.psum_scatter(
        (power_map * cluster_share).astype(jnp.bfloat16), "src", scatter_dimension=1, tiled=True
    ).astype(jnp.float32)
    return summed[:, None]


def gelu_of_half(v):
    c = 2.0 * math.sqrt(2.0 / math.pi)
    return v + v * jnp.tanh(v * (c + (c * 4.0 * 0.044715) * (v * v)))


def half_lanes(shape):
    return lax.broadcasted_iota(jnp.int32, shape, len(shape) - 1) < shape[-1] // 2


def pair_up(h, d, segs):
    n, sub, lanes = h.shape
    tile = 2 * sub
    pack = lambda v: v.reshape(-1, tile, lanes).astype(jnp.bfloat16)
    turn = lambda v: pltpu.roll(v, lanes // 2, 2)
    shape = (1, tile, lanes)
    low = half_lanes(shape)
    row = lax.broadcasted_iota(jnp.int32, shape, 1)
    if d * segs < sub:
        keep = (row % sub < sub // 2) == low
        other = pltpu.roll(h, sub // 2, 1)
        even = jnp.where(keep, pack(h), turn(pack(other)))
        odd = jnp.where(keep, pack(h[1 : n - 1]), turn(pack(other[1 : n - 1])))
        return odd, even
    if d * segs < tile:
        keep = (row < sub) == low
        full = jnp.concatenate([h[:1], h, h[n - 1 :]], axis=0)
        swapped = jnp.concatenate([full[i ^ 1 : (i ^ 1) + 1] for i in range(n + 2)], axis=0)
        own = jnp.where(keep, pack(full), turn(pack(swapped)))
        return own, own
    v = pack(h)
    turned = turn(v)
    g = d * segs // tile
    groups = v.shape[0] // g
    at = lambda x, m: x[m * g : (m + 1) * g]
    out = []
    for i in range((groups + 2) // 2):
        u, w = 2 * i - 1, 2 * i
        if i == 0:
            out += [at(turned, w), at(v, w)]
        elif w == groups:
            out += [at(v, u), at(turned, u)]
        else:
            out += [jnp.where(low, at(v, u), at(turned, w)), jnp.where(low, at(turned, u), at(v, w))]
    own = jnp.concatenate(out, axis=0)
    return own, own


def shift_segment(h, segs, down):
    sub = lax.broadcasted_iota(jnp.int32, (1,) + h.shape[1:], 1) % segs
    if down:
        return jnp.where(sub == 0, 0.0, pltpu.roll(h, 1, 1))
    return jnp.where(sub == segs - 1, 0.0, pltpu.roll(h, h.shape[1] - 1, 1))


MESH = pl.DeviceIdType.MESH
CHUNKS = 2


def xor(s, k):
    total = s
    bit = 1
    while bit <= k:
        if k & bit:
            total = total + bit - 2 * bit * ((s // bit) % 2)
        bit *= 2
    return total


def pixel_kernel(
    layers, n_src, f_arg, w_arg, h_arg, tr_arg, b_arg, y_arg, pw_arg, as_arg, o_ref, *scratch
):
    given = (f_arg, w_arg, h_arg, tr_arg, b_arg, y_arg, pw_arg, as_arg)
    *scratch, f_ref, w_ref, h_ref, tr_ref, b_ref, y_ref, pw_ref, as_ref, ls = scratch
    local = (f_ref, w_ref, h_ref, tr_ref, b_ref, y_ref, pw_ref, as_ref)
    fetch = [pltpu.make_async_copy(a, b, ls.at[i]) for i, (a, b) in enumerate(zip(given, local))]
    for copy in fetch:
        copy.start()
    first, bufs = scratch[0], (scratch[1 : layers + 1], scratch[layers + 1 : 2 * layers + 1])
    got, wraw, pbuf, mbuf, wide, acc, sbuf, obuf, stage, rowbuf, t_ref, m_ref = scratch[2 * layers + 1 : 2 * layers + 13]
    fs, fr, es, er, ws, wr, ys, yr, vs, vr, ps, pr, ms, mr, os, orr = scratch[2 * layers + 13 :]
    gp, s, c, r = (lax.axis_index(a) for a in ("grp", "src", "chan", "row"))
    lanes = t_ref.shape[2]
    half_rows = t_ref.shape[1]
    rows = 4 * half_rows
    piece = t_ref.shape[0] // 8
    here = 2 * c + r
    side = c

    barrier = pltpu.get_barrier_semaphore()
    for s1 in range(n_src):
        for c1 in range(2):
            for r1 in range(2):
                @pl.when(jnp.logical_not((s == s1) & (c == c1) & (r == r1)))
                def _():
                    pl.semaphore_signal(
                        barrier, inc=1, device_id={"src": s1, "chan": c1, "row": r1},
                        device_id_type=MESH,
                    )
    pl.semaphore_signal(barrier, inc=1, device_id={"grp": 1 - gp}, device_id_type=MESH)
    ch = lanes // 2
    fetch[0].wait()
    part, strip, block = f_ref.shape
    for ci in range(part):
        rowbuf[ci * strip : (ci + 1) * strip, :] = f_ref[ci].astype(jnp.float32)
    kin = lax.broadcasted_iota(jnp.int32, (block // 2, 2 * block), 1)
    kout = lax.broadcasted_iota(jnp.int32, (block // 2, 2 * block), 0)
    pick = jnp.where(kin % block == 2 * kout + kin // block, 1.0, 0.0).astype(jnp.bfloat16)
    blank = jnp.zeros((2 * part, block), jnp.bfloat16)
    base = part * strip
    for y4 in range(strip // 4):
        cells = []
        for y2 in (2 * y4, 2 * y4 + 1):
            both_rows = jnp.concatenate(
                [rowbuf[pl.ds(2 * y2 + yp, part, stride=strip), :] for yp in range(2)], axis=0
            ).astype(jnp.bfloat16)
            cells.append(jnp.concatenate([both_rows, blank], axis=1))
            cells.append(jnp.concatenate([blank, both_rows], axis=1))
        moved = lax.dot_general(
            pick, jnp.concatenate(cells, axis=0), (((1,), (1,)), ((), ())),
            preferred_element_type=jnp.float32)
        for e in range(2):
            rowbuf[pl.ds(base + 2 * y4 + e, block // 2, stride=half_rows), :] = moved[
                :, e * lanes : (e + 1) * lanes]
    for x8 in range(block // 16):
        t_ref[8 * x8 : 8 * x8 + 8] = rowbuf[
            base + 8 * x8 * half_rows : base + 8 * (x8 + 1) * half_rows, :
        ].reshape(8, half_rows, lanes).astype(t_ref.dtype)

    fetch[1].wait()
    per = layers // 2
    for l in range(layers):
        for i, (one, two) in enumerate(((1, 0), (4, 3), (7, 6), (2, 5), (8, None))):
            other = jnp.zeros((ch, ch), w_ref.dtype) if two is None else w_ref[l, two]
            wraw[0, l // per, (l % per) * 5 + i] = jnp.concatenate([w_ref[l, one], other], axis=1)

    for copy in fetch[2:]:
        copy.wait()
    planes2 = h_ref.shape[0]
    ia = lax.broadcasted_iota(jnp.int32, (planes2, planes2), 0)
    ib = lax.broadcasted_iota(jnp.int32, (planes2, planes2), 1)
    column = jnp.sum(jnp.where(ia == ib, tr_ref[...], 0.0), axis=1, keepdims=True)
    pbuf[0, :planes2, :] = jnp.concatenate(
        [h_ref[...].astype(jnp.float32), jnp.broadcast_to(column, (planes2, ch))], axis=1)
    bias_half = 0.5 * b_ref[...]
    pbuf[0, planes2 : planes2 + layers, :] = jnp.concatenate([bias_half, bias_half], axis=1)

    pl.semaphore_wait(barrier, 4 * n_src)

    def remote(src, dst, a, b, s1, c1, r1):
        return pltpu.make_async_remote_copy(
            src_ref=src, dst_ref=dst, send_sem=a, recv_sem=b,
            device_id={"src": s1, "chan": c1, "row": r1}, device_id_type=MESH,
        )

    def main_copy(c1, r1):
        return (
            t_ref.at[pl.ds(piece * (3 * c1 + 2 * r1), 3 * piece)],
            got.at[here, pl.ds(piece * (1 - c1), 3 * piece)],
        )

    def edge_copy(c1, r1):
        at = 7 * (1 - c1) if c1 == r1 else 1 + 5 * c1
        return t_ref.at[pl.ds(piece * at, piece)], got.at[here, pl.ds(piece * 3 * c1, piece)]

    def each(act):
        for c1 in (0, 1):
            for r1 in (0, 1):
                k = 2 * c1 + r1
                me = (c == c1) & (r == r1)
                act(c1, r1, k, me)

    def send_main(c1, r1, k, me):
        src, dst = main_copy(c1, r1)
        pl.when(jnp.logical_not(me))(
            lambda: remote(src, dst, fs.at[k], fr.at[here], s, c1, r1).start())
        pl.when(me)(lambda: pltpu.make_async_copy(src, dst, fr.at[here]).start())

    def edge_step(c1):
        return 1 - 2 * c1

    def send_edge(c1, r1, k, me):
        src, dst = edge_copy(c1, r1)
        if c1 == r1:
            s1 = s + edge_step(c1)
            pl.when((s1 >= 0) & (s1 < n_src))(
                lambda: remote(src, dst, es.at[k], er.at[here], s1, c1, r1).start())
        else:
            pl.when(jnp.logical_not(me))(
                lambda: remote(src, dst, es.at[k], er.at[here], s, c1, r1).start())
            pl.when(me)(lambda: pltpu.make_async_copy(src, dst, er.at[here]).start())

    def send_mask(c1, r1, k, me):
        src, dst = m_ref.at[k], mbuf.at[r]
        owner = c == (2 * s) // n_src
        pl.when(owner & jnp.logical_not(me))(
            lambda: remote(src, dst, ms.at[k], mr.at[r], s, c1, r1).start())
        pl.when(owner & me)(lambda: pltpu.make_async_copy(src, dst, mr.at[r]).start())

    each(send_main)
    each(send_edge)

    blocks = wraw.shape[2] // 2

    def wz(k):
        at = pl.ds(gp * blocks, blocks)
        return remote(wraw.at[0, r, at], wraw.at[k, r, at], ws.at[k], wr.at[k], xor(s, k), c, r)

    def wy(k, g1):
        piece_of = wraw.at[k, r, pl.ds(g1 * blocks, blocks)]
        return pltpu.make_async_remote_copy(
            src_ref=piece_of, dst_ref=piece_of, send_sem=ys.at[k], recv_sem=yr.at[k],
            device_id={"grp": 1 - gp}, device_id_type=MESH,
        )

    def pz(k):
        return remote(pbuf.at[0], pbuf.at[k], ps.at[k], pr.at[k], xor(s, k), c, r)

    for k in range(1, n_src):
        pz(k).start()
        wz(k).start()
    column = pl.multiple_of((s % (y_ref.shape[1] // block)) * block, block)
    wanted = y_ref[:, pl.ds(column, block)].astype(jnp.bfloat16)
    unit = half_rows // 2
    xin = lax.broadcasted_iota(jnp.int32, (block, block), 0)
    xout = lax.broadcasted_iota(jnp.int32, (block, block), 1)
    from_x = xout // (4 * unit) * (4 * unit) + (xout // unit % 2) * 2 * unit + (xout // (2 * unit) % 2) * unit + xout % unit
    sorted_x = jnp.dot(
        wanted, jnp.where(xin == from_x, 1.0, 0.0).astype(jnp.bfloat16), preferred_element_type=jnp.float32)
    seg_of = lax.broadcasted_iota(jnp.int32, (8, block), 1) // (block // 8)
    sub_of = lax.broadcasted_iota(jnp.int32, (8, block), 0)
    for g in range(strip // 8):
        tile = sorted_x[8 * g : 8 * g + 8]
        turned = tile
        for e in range(1, 8):
            moved = pltpu.roll(pltpu.roll(tile, 8 - e, 0), e * block // 8, 1)
            turned = jnp.where((seg_of - sub_of + 8) % 8 == e, moved, turned)
        for kt in range(4):
            m_ref[kt, 2 * g : 2 * g + 2, :] = turned[2 * kt : 2 * kt + 2]
    each(send_mask)

    for k in range(n_src):
        for l in range(layers):
            for at, cut in ((0, lanes), (12 * ch, 0)):
                wide[k, l, at : at + 4 * ch, cut : cut + lanes] = jnp.zeros((4 * ch, lanes), wide.dtype)
    outside = ((here == 0) & (s == 0)) | ((here == 3) & (s == n_src - 1))

    @pl.when(outside)
    def _():
        for k in range(4):
            got[k, pl.ds(piece * 3 * side, piece)] = jnp.zeros((piece,) + got.shape[2:], got.dtype)

    def build(k):
        low = lax.broadcasted_iota(jnp.int32, (ch, lanes), 1) < ch
        per = layers // 2
        for l in range(layers):
            raw = lambda i: wraw[k, l // per, (l % per) * 5 + i].astype(jnp.float32) * 0.5
            firsts = [raw(b) for b in range(3)]
            q0, q1 = raw(3), raw(4)
            seconds = [q0, pltpu.roll(q0, ch, 1), q1]
            for b in range(3):
                w10, w2 = firsts[b], seconds[b]
                swap = pltpu.roll(w10, ch, 1)
                blocks = [
                    w10,
                    jnp.where(low, w2, swap),
                    jnp.where(low, 0.0, pltpu.roll(w2, ch, 1)),
                    jnp.where(low, swap, 0.0),
                ]
                for j in range(4):
                    v = blocks[j].astype(wide.dtype)
                    for ic in range(2):
                        at = (b + ic) * 4 * ch + j * ch
                        wide[k, l, at : at + ch, ic * lanes : (ic + 1) * lanes] = v

    build(0)

    def wait_main(c1, r1, k, me):
        src, _ = main_copy(0, 0)
        dst = got.at[k, pl.ds(piece * (1 - side), 3 * piece)]
        pl.when(jnp.logical_not(me))(
            lambda: remote(src, dst, fs.at[k], fr.at[k], s, c1, r1).wait_recv())
        pl.when(me)(lambda: pltpu.make_async_copy(src, dst, fr.at[k]).wait())

    def wait_edge(c1, r1, k, me):
        src, _ = edge_copy(0, 0)
        dst = got.at[k, pl.ds(piece * 3 * side, piece)]
        far = c == r
        inside = jnp.logical_not(outside)
        pl.when(jnp.where(far, inside, jnp.logical_not(me)))(
            lambda: remote(src, dst, es.at[k], er.at[k], s, c1, r1).wait_recv())
        pl.when(jnp.logical_not(far) & me)(
            lambda: pltpu.make_async_copy(src, dst, er.at[k]).wait())

    def take(k):
        wz(k).wait_recv()
        wy(k, gp).start()

    take(1)
    each(wait_main)
    each(wait_edge)
    q = ch // 2
    span = 2**layers
    segs = rows // span
    slots = got.shape[1]
    own_cols = 2 * slots - 2 * span
    rin = lax.broadcasted_iota(jnp.int32, (2 * lanes, 2 * lanes), 0)
    rout = lax.broadcasted_iota(jnp.int32, (2 * lanes, 2 * lanes), 1)
    want = (rout // q % 2) * lanes + (rout // ch % 2) * ch + (rout // lanes) * q + rout % q
    place = jnp.where(rin == want, 1.0, 0.0).astype(t_ref.dtype)
    for r1 in range(2):
        lhs = jnp.concatenate(
            [got[2 * c1 + r1].reshape(slots * half_rows, lanes) for c1 in range(2)], axis=1)
        v = jnp.dot(lhs, place, preferred_element_type=jnp.float32)
        for yp in range(2):
            stage[2 * r1 + yp] = v[:, yp * lanes : (yp + 1) * lanes]
    mrows = slots * segs
    rowbuf[0:8, :] = jnp.zeros((8, lanes), jnp.float32)
    rowbuf[8 + span * mrows : 16 + span * mrows, :] = jnp.zeros((8, lanes), jnp.float32)
    for r1 in range(2):
        for y2 in range(half_rows):
            for yp in range(2):
                y = 2 * y2 + yp
                at = 8 + (y % span) * mrows + r1 * (segs // 2) + y // span
                rowbuf[pl.ds(at, slots, stride=segs), :] = stage[
                    2 * r1 + yp, pl.ds(y2, slots, stride=half_rows), :]
    low_lanes = half_lanes((1, 8, lanes))
    as_tiles = lambda v: v.reshape(-1, 8, lanes)
    for y in range(span):
        at = 8 + y * mrows
        own = as_tiles(rowbuf[at : at + mrows, :])
        near = jnp.where(
            low_lanes, as_tiles(rowbuf[at + segs : at + segs + mrows, :]),
            as_tiles(rowbuf[at - segs : at - segs + mrows, :]))
        places = [(y, own, near)]
        if y == span - 1:
            places.append((-1, shift_segment(own, segs, True), shift_segment(near, segs, True)))
        if y == 0:
            places.append((span, shift_segment(own, segs, False), shift_segment(near, segs, False)))
        for yy, a, b in places:
            first[yy + 1, :, :lanes] = a.reshape(mrows, lanes).astype(first.dtype)
            first[yy + 1, :, lanes:] = b.reshape(mrows, lanes).astype(first.dtype)

    at_left = (here == 0) & (s == 0)
    at_right = (here == 3) & (s == n_src - 1)
    for r1 in range(2):
        for_self = (c == (2 * s) // n_src) & (r == r1)
        pl.when(jnp.logical_not(for_self))(
            lambda: remote(m_ref.at[0], mbuf.at[r1], ms.at[0], mr.at[r1], s, c, r).wait_recv())
        pl.when(for_self)(
            lambda: pltpu.make_async_copy(m_ref.at[0], mbuf.at[r1], mr.at[r1]).wait())

    def share_copy(k):
        return remote(wraw.at[k, r], wraw.at[k, r], vs.at[k], vr.at[k], s, c, 1 - r)

    total = jnp.sum(pw_ref[...], axis=1, keepdims=True)

    low_tile = half_lanes((1, 16, lanes))
    outside_tiles = (slots // 2 - own_cols // 4) * segs // 16

    def bordered(v):
        n = v.shape[0]
        missing = mrows // 16 - n
        zero = jnp.zeros((), v.dtype)
        if missing:
            half = lax.broadcasted_iota(jnp.int32, (1, 16, lanes), 1) < 8
            left = [jnp.where(at_left, zero, v[: outside_tiles - 1]),
                    jnp.where(at_left & half, zero, v[outside_tiles - 1 : outside_tiles])]
            right = [jnp.where(at_right & jnp.logical_not(half), zero, v[n - outside_tiles : n - outside_tiles + 1]),
                     jnp.where(at_right, zero, v[n - outside_tiles + 1 :])]
            middle = [v[outside_tiles : n - outside_tiles]]
            return jnp.concatenate(left + middle + right, axis=0)
        return jnp.concatenate(
            [jnp.where(at_left, zero, v[:outside_tiles]), v[outside_tiles : n - outside_tiles],
             jnp.where(at_right, zero, v[n - outside_tiles :])], axis=0)

    def store_next(dst, h, y, d):
        wider = 2 * d
        places = [(y, h)]
        if y >= span - wider:
            places.append((y - span, shift_segment(h, segs, True)))
        if y < wider:
            places.append((y + span, shift_segment(h, segs, False)))
        for yy, v in places:
            own, around = pair_up(v, d, segs)
            around = bordered(around)
            if own.shape[0] != around.shape[0]:
                own = bordered(own)
                near = jnp.where(low_tile, around[1:], around[:-1])
            else:
                g = wider * segs // 16
                own = around[g : around.shape[0] - g]
                near = jnp.where(low_tile, around[2 * g :], around[: around.shape[0] - 2 * g])
            dst[yy + wider, :, :lanes] = own.reshape(-1, lanes)
            dst[yy + wider, :, lanes:] = near.reshape(-1, lanes)

    def multiply(k, l, ys):
        d = 2**l
        src = first if l == 0 else bufs[k % 2][l - 1]
        lhs = jnp.concatenate(
            [jnp.concatenate([src[y + j * d] for y in ys], axis=0) for j in range(4)], axis=1)
        return jnp.dot(lhs, wide[k, l], preferred_element_type=jnp.float32)

    def activate(k, l, ys, out):
        d = 2**l
        src = first if l == 0 else bufs[k % 2][l - 1]
        dst = bufs[k % 2][l]
        n = src.shape[1]
        bias = pbuf[k, 2 * q2 + l : 2 * q2 + l + 1, :]
        for i, y in enumerate(ys):
            for e in range(2):
                z = out[i * n : (i + 1) * n, e * lanes : (e + 1) * lanes] + bias
                yy = y + e * d
                h = src[yy + d, :, :lanes].astype(jnp.float32) + gelu_of_half(z)
                if l + 1 < layers:
                    store_next(dst, h.reshape(-1, 8, lanes), yy, d)
                else:
                    dst[yy * n : (yy + 1) * n, :] = h

    def finish(k, cid):
        share = jnp.sum(jnp.where(as_ref[...] == cid, pw_ref[...], 0.0), axis=1, keepdims=True) / total
        final = bufs[k % 2][layers - 1]
        n = final.shape[0] // span
        head = pbuf[k, : 2 * q2, :]
        low = lax.broadcasted_iota(jnp.int32, head.shape, 1) < ch
        h_lo = jnp.where(low, head, 0.0)
        h_hi = jnp.where(low, 0.0, pltpu.roll(head, ch, 1))
        tcol = head[:, ch : ch + 1]
        hw = jnp.concatenate([h_lo[:q2], h_hi[:q2], h_lo[q2:], h_hi[q2:]], axis=0).astype(jnp.bfloat16)
        tr = jnp.concatenate([tcol[:q2], tcol[:q2], tcol[q2:], tcol[q2:]], axis=0)
        per = rows // 16
        for g in range(rows // 8):
            at = 8 * (g % 2) * n + g // 2
            block = jnp.concatenate(
                [final[pl.ds(at + b * n, n // segs, stride=segs), :] for b in range(8)], axis=0
            ).astype(jnp.bfloat16)
            field = lax.dot_general(
                hw, block, (((1,), (1,)), ((), ())), preferred_element_type=jnp.float32)
            m = mbuf[g // per, 2 * (g % per) : 2 * (g % per) + 2]
            mm = jnp.concatenate(
                [jnp.broadcast_to(m[i : i + 1], (q2, m.shape[1])) for i in (0, 1, 0, 1)], axis=0)
            field = field + mm * tr
            power = (field[: 2 * q2] ** 2 + field[2 * q2 :] ** 2) * share
            if k == 0:
                acc[g] = power
            else:
                acc[g] = acc[g] + power

    q2 = h_ref.shape[0] // 2

    def cross(k):
        wy(k, 1 - gp).wait_recv()
        share_copy(k).start()

    def receive(k):
        remote(
            wraw.at[k, 1 - r], wraw.at[k, 1 - r], vs.at[k], vr.at[k], s, c, 1 - r
        ).wait_recv()
        pz(k).wait_recv()
        build(k)

    tops = lambda d: [y for y in range(span) if y % (2 * d) < d]
    ahead = layers // 2
    cross(1)
    take(2)
    pending = None
    for step in range(ahead * (n_src + 1)):
        k0, l0 = step // ahead, step % ahead
        if l0 == 0 and 0 < k0 < n_src:
            receive(k0)
        if l0 == 0 and k0 + 1 < n_src and k0:
            cross(k0 + 1)
            if k0 + 2 < n_src:
                take(k0 + 2)
        for k, l in ((k0, l0), (k0 - 1, l0 + ahead)):
            if not 0 <= k < n_src:
                continue
            ys_all = tops(2**l)
            count = len(ys_all) // CHUNKS
            for i in range(CHUNKS):
                some = ys_all[i * count : (i + 1) * count]
                if pending and pending[0] == k and pending[1] != l:
                    activate(*pending)
                    pending = None
                out = multiply(k, l, some)
                if pending:
                    activate(*pending)
                pending = (k, l, some, out)
        if l0 == ahead - 1 and k0:
            if pending[0] == k0 - 1:
                activate(*pending)
                pending = None
            finish(k0 - 1, xor(s, k0 - 1))

    pin = lax.broadcasted_iota(jnp.int32, (2 * lanes, 2 * lanes), 0)
    pout = lax.broadcasted_iota(jnp.int32, (2 * lanes, 2 * lanes), 1)
    column = pout % own_cols
    half = span // 2
    source = (
        (column // half % 2) * lanes + pout // own_cols * (own_cols // 2)
        + column // span * half + column % half)
    order = jnp.where(pin == source, 1.0, 0.0).astype(jnp.bfloat16)
    both = jnp.concatenate(
        [jnp.concatenate([acc[g, :q2], acc[g, q2:]], axis=1) for g in range(rows // 8)], axis=0)
    sbuf[...] = jnp.dot(
        both.astype(jnp.bfloat16), order, preferred_element_type=jnp.float32
    ).reshape(sbuf.shape)

    c2 = (2 * s) // n_src
    slot = 4 * (s % 2) + here

    def outgoing(act):
        for s1 in range(n_src):
            for r1 in range(2):
                k = 2 * s1 + r1
                src = sbuf.at[n_src * r1 + s1]
                me = (s == s1) & (c == c2) & (r == r1)
                act(s1, r1, k, src, me)

    def send_out(s1, r1, k, src, me):
        dst = obuf.at[slot]
        pl.when(jnp.logical_not(me))(
            lambda: remote(src, dst, os.at[k], orr.at[slot], s1, c2, r1).start())
        pl.when(me)(lambda: pltpu.make_async_copy(src, dst, orr.at[slot]).start())

    outgoing(send_out)
    mine = c == c2
    for k in range(2 * n_src):
        me = mine & (slot == k)
        src = sbuf.at[0]
        pl.when(jnp.logical_not(me))(
            lambda: remote(src, obuf.at[k], os.at[k], orr.at[k], s, c, r).wait_recv())
        pl.when(me)(lambda: pltpu.make_async_copy(src, obuf.at[k], orr.at[k]).wait())
    for b in range(8):
        o_ref[:, b, :] = jnp.concatenate(
            [obuf[k, :, b * own_cols : (b + 1) * own_cols] for k in range(2 * n_src)], axis=1)

    def sent_main(c1, r1, k, me):
        src, dst = main_copy(c1, r1)
        pl.when(jnp.logical_not(me))(
            lambda: remote(src, dst, fs.at[k], fr.at[here], s, c1, r1).wait_send())

    def sent_edge(c1, r1, k, me):
        src, dst = edge_copy(c1, r1)
        s1 = s + edge_step(c1)
        gone = (s1 >= 0) & (s1 < n_src) if c1 == r1 else jnp.logical_not(me)
        pl.when(gone)(lambda: remote(src, dst, es.at[k], er.at[here], s, c1, r1).wait_send())

    def sent_mask(c1, r1, k, me):
        owner = c == (2 * s) // n_src
        pl.when(owner & jnp.logical_not(me))(
            lambda: remote(m_ref.at[k], mbuf.at[r], ms.at[k], mr.at[r], s, c1, r1).wait_send())

    def sent_out(s1, r1, k, src, me):
        pl.when(jnp.logical_not(me))(
            lambda: remote(src, obuf.at[slot], os.at[k], orr.at[slot], s1, c2, r1).wait_send())

    each(sent_main)
    each(sent_edge)
    each(sent_mask)
    outgoing(sent_out)
    for k in range(1, n_src):
        pz(k).wait_send()
        wz(k).wait_send()
        wy(k, gp).wait_send()
        share_copy(k).wait_send()


def by_pixel(
    features, layout, conv_weight, conv_bias, head_weight, transmission, point_weight, assignment
):
    n_src, n_chan, n_row = (lax.axis_size(a) for a in ("src", "chan", "row"))
    layers = conv_weight.shape[1]
    part, strip, block = features.shape
    ch = part * n_chan
    width = block * n_src
    rows = strip * n_row
    own = block // (n_chan * n_row)
    lanes = 2 * ch
    span = 2**layers
    planes2 = head_weight.shape[2]
    spec = lambda shape, kind=jnp.bfloat16: pltpu.VMEM(shape, kind)
    scratch = []
    slots = block // 4
    segs = rows // span
    scratch.append(spec((span + 2, slots * segs, 2 * lanes)))
    for _ in range(2):
        for l in range(1, layers):
            scratch.append(spec((span + 2 * 2**l, (slots - 2 * 2**l) * segs, 2 * lanes)))
        scratch.append(spec((span * (slots - span) * segs, lanes), jnp.float32))
    groups = rows // 8
    scratch += [
        spec((4, slots, strip // 2, lanes)),
        spec((n_src, 2, layers // 2 * 5, ch, lanes)),
        spec((n_src, planes2 + (layers + 7) // 8 * 8, lanes), jnp.float32),
        spec((2, strip // 4, block), jnp.float32),
        spec((n_src, layers, 16 * ch, 2 * lanes)),
        spec((groups, planes2, lanes), jnp.float32),
        spec((groups, planes2 // 2, 8 * own), jnp.float32),
        spec((2 * n_src, planes2 // 2, 8 * own), jnp.float32),
        spec((4, slots * strip // 2, lanes), jnp.float32),
        spec((span * slots * segs + 16, lanes), jnp.float32),
        spec((block // 2, strip // 2, lanes)),
        spec((4, strip // 4, block), jnp.float32),
    ]
    dma = pltpu.SemaphoreType.DMA
    given = (features, conv_weight[0], head_weight[0].T, transmission, conv_bias[0], layout, point_weight[None], assignment.reshape(1, -1))
    for count in (4, 4, 4, 4, n_src, n_src, n_src, n_src, n_src, n_src, n_src, n_src, 4, 2, 2 * n_src, 2 * n_src):
        scratch.append(dma((count,)))
    scratch += [spec(a.shape, a.dtype) for a in given] + [dma((len(given),))]
    vmem = pl.BlockSpec(memory_space=pltpu.VMEM)
    out = pl.pallas_call(
        functools.partial(pixel_kernel, layers, n_src),
        out_shape=jax.ShapeDtypeStruct((planes2 // 2, 8, width // n_chan), jnp.float32),
        in_specs=[pl.BlockSpec(memory_space=pltpu.HBM)] * len(given),
        out_specs=vmem,
        scratch_shapes=scratch,
        compiler_params=pltpu.CompilerParams(
            vmem_limit_bytes=67043328 - 66 * 1024, collective_id=0, has_side_effects=True),
    )(*given)
    return out[:, None]


def solution(mesh):
    in_specs = (
        P("chan", ("grp", "row"), "src"),
        P(("grp", "row"), "chan"),
        P("src", None, None, None, None),
        P("src", None, None),
        P("src", None, None),
        P("src", None),
        P(),
        P(),
    )
    out_specs = P(None, ("grp", "row"), "src", "chan")

    def shards(*args):
        features, weights = args[0], args[2]
        halo = 2 ** weights.shape[1] - 1
        own = features.shape[2] // (mesh.shape["chan"] * mesh.shape["row"])
        fits = own >= 2 * halo and mesh.shape["chan"] == mesh.shape["row"] == 2
        body = by_pixel if fits and mesh.shape["src"] == 4 and mesh.shape["grp"] == 2 else by_cluster
        return body(*args)

    return jax.shard_map(shards, mesh=mesh, in_specs=in_specs, out_specs=out_specs, check_vma=False)
```
